32 devices in a mesh: groups: 2 (over x), expert: 8 (over z, y), attn: 2 (over core).
Axes of the slice: x: 2, y: 2, z: 4, core: 2. Of those that a mesh axis runs over, the one named last changes fastest.
Arguments:
- queries: bfloat16 [4096, 2048], P(('groups', 'expert'), 'attn'), parts along dimension 0, may hold values from -180 to 180
- new_keys: bfloat16 [4096, 256], P(('groups', 'expert'), 'attn'), parts along dimension 0, may hold values from -6 to 6
- new_values: bfloat16 [4096, 256], P(('groups', 'expert'), 'attn'), parts along dimension 0, may hold values from -6 to 6
- cache_keys: bfloat16 [32, 1024, 256], P(('groups', 'expert'), None, 'attn'), parts along dimension 0, may hold values from -6 to 6
- cache_values: bfloat16 [32, 1024, 256], P(('groups', 'expert'), None, 'attn'), parts along dimension 0, may hold values from -6 to 6
- cache_len: int32 [32], P(('groups', 'expert')), parts along dimension 0, may hold values from 1 to 1024, as said below
- span_req: int32 [32], P(('groups', 'expert')), parts along dimension 0, may hold values from 0 to 15, as said below
- out_proj: bfloat16 [2048, 2048], P('attn'), may hold values from -0.5 to 0.5
- resid: bfloat16 [4096, 2048], P(('groups', 'expert', 'attn')), parts along dimension 0, may hold values from -60 to 60
- norm_gain: float32 [2048], replicated, may hold values from 0.1 to 1.9
- routes: int32 [4096, 8], P(('groups', 'expert', 'attn')), parts along dimension 0, may hold values from 0 to 15, all different within a row; in each aligned block of 128 rows (0 to 127, 128 to 255, ...) at most 128 rows name the same one
- gates: float32 [4096, 8], P(('groups', 'expert', 'attn')), parts along dimension 0, may hold values from 0.05 to 1
- w_gate: bfloat16 [16, 2048, 384], P(('expert', 'attn')), may hold values from -0.125 to 0.125
- w_up: bfloat16 [16, 2048, 384], P(('expert', 'attn')), may hold values from -0.125 to 0.125
- w_down: bfloat16 [16, 384, 2048], P(('expert', 'attn')), may hold values from -0.3125 to 0.3125
Outputs:
- layer_out: bfloat16 [4096, 2048], P(('groups', 'expert', 'attn')), parts along dimension 0
The draws below stay inside these ranges and needn't reach their ends.
There are 2 independent parts, one for each index of `groups`. The reference program is written for one: setup_inputs(seed, part) draws one part's arguments, and reference() takes and returns one part's arrays. A program takes and returns all parts, laid end to end along the dimension named above; an argument that names none is the same for every part. Nothing has to cross between parts.
Inputs may be any that keep to these rules, and one draw needn't show every extreme that they name: `cache_len`: some request has exactly 1024 cached tokens. `span_req`: the 2 spans c with c // 2 = b belong to the 2 distinct requests b * 2 to (b + 1) * 2 - 1. `routes`: among the 128 tokens of one device no expert is named more than 128 times.
All inputs are finite; a program needn't handle non-finite values.
Results may differ from the reference program's by a relative error of at most 0.0054.
Values may be sent and summed in bfloat16 or wider, within the bound.
No kernel may reach another device: no remote copies, remote signals or barrier semaphores. Data moves between devices by JAX's collectives and lax.ppermute only.
A program may use at most 128 MiB of HBM per device.

```python
import math
import jax
import jax.numpy as jnp
import numpy as np
from jax import lax

D = 2048
QH = 16
KVH = 2
HD = 128
FF = 384
TOPK = 8
LEN_SPAN = 128
REQ_DEV = 2
CACHE = 1024
ROWS_DEV = 128
REQUESTS = 16
TOKENS = 2048
EXPERTS = 16
CAP = 128


def shared_attention(key):
    keys_drawn = jnp.clip(jax.random.normal(jax.random.fold_in(key, 11), (TOKENS, KVH * HD), jnp.float32), -6.0, 6.0)
    queries_drawn = jnp.clip(jax.random.normal(jax.random.fold_in(key, 12), (TOKENS, QH * HD), jnp.float32), -6.0, 6.0)
    return (queries_drawn, keys_drawn)


def draw_queries(key, part):
    return shared_attention(key)[0].astype(jnp.bfloat16)


def draw_new_keys(key, part):
    return shared_attention(key)[1].astype(jnp.bfloat16)


def draw_resid(key, part):
    base = jnp.clip(jax.random.normal(jax.random.fold_in(key, 41), (TOKENS, D), jnp.float32), -6.0, 6.0)
    return base.astype(jnp.bfloat16)


def draw_cache_len(key, part):
    lengths = jax.random.randint(jax.random.fold_in(key, 21), (REQUESTS,), 1, CACHE + 1, jnp.int32)
    chosen = jax.random.randint(jax.random.fold_in(key, 22), (), 0, REQUESTS, jnp.int32)
    return lengths.at[chosen].set(CACHE)


def draw_span_req(key, part):
    blocks = REQUESTS // REQ_DEV
    ranking = jax.random.randint(jax.random.fold_in(key, 31), (blocks, REQ_DEV), 0, 1 << 20, jnp.int32)
    ranking = ranking * REQ_DEV + jnp.arange(REQ_DEV, dtype=jnp.int32)[None, :]
    ordering = jnp.argsort(ranking, axis=1, stable=True).astype(jnp.int32)
    return (ordering + (jnp.arange(blocks, dtype=jnp.int32) * REQ_DEV)[:, None]).reshape(-1)


def block_scale(stream_key, extent, split, smallest, top_value):
    loudness, own = 1.0, jax.random.fold_in(stream_key, 6)
    for axis_at, shards_of in split:
        draws = jnp.exp(jax.random.uniform(jax.random.fold_in(own, axis_at), (shards_of,), jnp.float32, smallest / len(split), top_value / len(split)))
        loudness = loudness * jnp.repeat(draws, extent[axis_at] // shards_of).reshape([-1 if axis == axis_at else 1 for axis in range(len(extent))])
    return loudness


def deal_out(own_key, own, number, rows, amount, top, bound, lean):
    order = jax.random.permutation(own_key, amount)
    heavy_load, ordinary = shares(amount, rows * top, bound, lean, True), shares(amount, rows * top, bound, lean, False)
    places = jnp.arange(amount)

    def named(sizes, turn):
        used = int((sizes > 0).sum())
        fixed = max(1, used // 4)
        moved = fixed + (places - fixed + turn * (used - fixed)) % max(1, amount - fixed)
        return jnp.zeros((amount,), jnp.int32).at[order[jnp.where(places < fixed, places, moved)]].set(jnp.asarray(sizes, jnp.int32))

    sizes = jnp.where(number % 4 == 0, named(heavy_load, number // 4), named(ordinary, number - number // 4 - 1))
    mixed = jax.random.permutation(jax.random.fold_in(own, 3), amount)
    giver, sink = mixed[0:amount // 2 * 2:2], mixed[1:amount // 2 * 2:2]
    room = jnp.minimum(sizes[giver] - 1, bound - sizes[sink]) // 2
    room = jnp.where((giver == order[0]) | (sink == order[0]) | (sizes[sink] == 0), 0, jnp.maximum(room, 0))
    moved = jax.random.randint(jax.random.fold_in(own, 4), (amount // 2,), 0, 1 << 20) % (room + 1)
    sizes = sizes.at[giver].add(-moved).at[sink].add(moved)
    labels = jnp.searchsorted(jnp.cumsum(sizes), jnp.arange(rows * top), side="right").astype(jnp.int32)
    table = labels.reshape(top, rows).T
    table = table[jax.random.permutation(jax.random.fold_in(own, 1), rows)]
    turn = jax.random.randint(jax.random.fold_in(own, 2), (rows, 1), 0, top)
    return jnp.take_along_axis(table, (jnp.arange(top)[None, :] + turn) % top, axis=1)


def shares(amount, total, most, skew, full):
    weights = [(1 << 20) // math.isqrt(standing ** skew) + 1 for standing in range(1, amount + 1)]
    largest = most if full else min(most, max(-(-total // amount), total * weights[0] // sum(weights)))
    least = 1 if total - largest >= amount - 1 else 0
    given, surplus = [largest] + [least] * (amount - 1), total - largest - least * (amount - 1)
    while surplus > 0:
        candidates = [i for i in range(1, amount) if given[i] < largest] or [i for i in range(1, amount) if given[i] < most]
        mass, budget = sum([weights[i] for i in candidates]), surplus
        for i in candidates:
            extra = min(most - given[i], max(1, budget * weights[i] // mass), surplus)
            given[i] = given[i] + extra
            surplus = surplus - extra
    return np.array(given)


def gaussian(stream_key, shape, spread, bound, cuts=(), kind=jnp.bfloat16):
    values = jax.random.normal(stream_key, shape, jnp.float32) * spread
    if len(cuts) > 0:
        values = block_scale(stream_key, shape, cuts, -0.22, 0.18) * values
    return jnp.clip(values, min=-bound, max=bound).astype(kind)


def setup_inputs(seed: int = 0, part: int = 0) -> dict:
    splits = jax.random.split(jax.random.key(seed), 16)
    part_splits = jax.random.split(jax.random.fold_in(splits[15], part), 16)
    queries = draw_queries(jax.random.fold_in(jax.random.fold_in(splits[15], part), 71), part)
    new_keys = draw_new_keys(jax.random.fold_in(jax.random.fold_in(splits[15], part), 71), part)
    new_values = gaussian(part_splits[2], (TOKENS, KVH * HD), 1.0, 6.0, ((0, 8), (1, 2)))
    cache_keys = gaussian(part_splits[3], (REQUESTS, CACHE, KVH * HD), 1.0, 6.0, ((0, 8), (2, 2)))
    cache_values = gaussian(part_splits[4], (REQUESTS, CACHE, KVH * HD), 1.0, 6.0, ((0, 8), (2, 2)))
    cache_len = draw_cache_len(jax.random.fold_in(jax.random.fold_in(splits[15], part), 71), part)
    span_req = draw_span_req(jax.random.fold_in(jax.random.fold_in(splits[15], part), 71), part)
    out_proj = gaussian(splits[7], (QH * HD, D), (QH * HD // 16) ** -0.5, 0.5, ((0, 2),))
    resid = draw_resid(jax.random.fold_in(jax.random.fold_in(splits[15], part), 71), part)
    norm_gain = jnp.clip(1.0 + 0.18 * jax.random.normal(splits[9], (D,), jnp.float32), 0.1, 1.9)
    routes_keys = jax.random.split(jax.random.fold_in(part_splits[10], 1), TOKENS // ROWS_DEV)
    routes_turns = jax.random.permutation(jax.random.fold_in(part_splits[10], 3), TOKENS // ROWS_DEV)
    routes = jax.vmap(lambda own, number: deal_out(jax.random.fold_in(part_splits[10], 2), own, number, ROWS_DEV, EXPERTS, TOPK, CAP, 2))(routes_keys, routes_turns).reshape((TOKENS, TOPK))
    gates = jnp.clip(jnp.exp(math.log(1.0) - 2.9957323 * jax.random.uniform(part_splits[11], (TOKENS, TOPK), jnp.float32) ** block_scale(part_splits[11], (TOKENS, TOPK), ((0, 16),), -0.2, 0.2)), 0.05, 1.0)
    w_gate = gaussian(splits[12], (EXPERTS, D, FF), D ** -0.5, 0.125, ((0, 16),))
    w_up = gaussian(splits[13], (EXPERTS, D, FF), D ** -0.5, 0.125, ((0, 16),))
    w_down = gaussian(splits[14], (EXPERTS, FF, D), FF ** -0.5, 0.3125, ((0, 16),))
    return dict(queries=queries, new_keys=new_keys, new_values=new_values, cache_keys=cache_keys, cache_values=cache_values, cache_len=cache_len, span_req=span_req, out_proj=out_proj, resid=resid, norm_gain=norm_gain, routes=routes, gates=gates, w_gate=w_gate, w_up=w_up, w_down=w_down)


negative_fill = -1e+30

def attend_span(query_rows, own_keys, own_values, keys_cached, values_cached, cache_length):
    group_size = QH // KVH
    queries_split = query_rows.reshape(LEN_SPAN, KVH, group_size, HD).astype(jnp.float32)
    all_keys = jnp.concatenate([keys_cached, own_keys], axis=0).reshape(CACHE + LEN_SPAN, KVH, HD).astype(jnp.float32)
    all_values = jnp.concatenate([values_cached, own_values], axis=0).reshape(CACHE + LEN_SPAN, KVH, HD).astype(jnp.float32)
    scores = jnp.einsum('lgqd,kgd->gqlk', queries_split, all_keys) * (1.0 / math.sqrt(HD))
    key_pos = jnp.arange(CACHE + LEN_SPAN, dtype=jnp.int32)
    query_pos = jnp.arange(LEN_SPAN, dtype=jnp.int32)
    in_cache = jnp.broadcast_to(key_pos[None, :] < cache_length, (LEN_SPAN, CACHE + LEN_SPAN))
    own_seen = key_pos[None, :] - CACHE <= query_pos[:, None]
    visible = jnp.where(key_pos[None, :] < CACHE, in_cache, own_seen)
    scores = jnp.where(visible[None, None], scores, negative_fill)
    weights = jax.nn.softmax(scores, axis=-1).astype(jnp.bfloat16)
    attended = jnp.einsum('gqlk,kgd->lgqd', weights.astype(jnp.float32), all_values)
    return attended.astype(jnp.bfloat16).reshape(LEN_SPAN, QH * HD)

def reference(queries, new_keys, new_values, cache_keys, cache_values, cache_len, span_req, out_proj, resid, norm_gain, routes, gates, w_gate, w_up, w_down):

    def one_span(span):
        request = span_req[span].astype(jnp.int32)
        first_row = (span * LEN_SPAN).astype(jnp.int32)
        query_rows = lax.dynamic_slice_in_dim(queries, first_row, LEN_SPAN, 0)
        own_keys = lax.dynamic_slice_in_dim(new_keys, first_row, LEN_SPAN, 0)
        own_values = lax.dynamic_slice_in_dim(new_values, first_row, LEN_SPAN, 0)
        keys_cached = lax.dynamic_index_in_dim(cache_keys, request, 0, keepdims=False)
        values_cached = lax.dynamic_index_in_dim(cache_values, request, 0, keepdims=False)
        return attend_span(query_rows, own_keys, own_values, keys_cached, values_cached, cache_len[request])
    attended = lax.map(one_span, jnp.arange(REQUESTS, dtype=jnp.int32)).reshape(TOKENS, QH * HD)
    attn_out = jnp.dot(attended, out_proj, preferred_element_type=jnp.float32)
    hidden = (resid.astype(jnp.float32) + attn_out).astype(jnp.bfloat16)
    state_float = hidden.astype(jnp.float32)
    mean_square = lax.optimization_barrier(jnp.mean(state_float * state_float, axis=-1, keepdims=True))
    normed = (state_float * lax.rsqrt(mean_square + 1e-06) * norm_gain.astype(jnp.float32)).astype(jnp.bfloat16)
    weight = gates / lax.optimization_barrier(jnp.sum(gates, axis=-1, keepdims=True))
    flat_routes = routes.reshape(-1)
    flat_weight = jnp.concatenate([weight.reshape(-1), jnp.zeros((1,), jnp.float32)])
    padded_rows = jnp.concatenate([normed, jnp.zeros((1, D), jnp.bfloat16)], axis=0)

    def expert_step(accum_out, expert_id):
        pair_index = jnp.nonzero(flat_routes == expert_id, size=EXPERTS * CAP, fill_value=TOKENS * TOPK)[0].astype(jnp.int32)
        token_index = pair_index // TOPK
        rows_in = padded_rows[token_index]
        gate_part = jnp.dot(rows_in, w_gate[expert_id], preferred_element_type=jnp.float32)
        up_part = jnp.dot(rows_in, w_up[expert_id], preferred_element_type=jnp.float32)
        act = (jax.nn.silu(gate_part) * up_part).astype(jnp.bfloat16)
        expert_out = jnp.dot(act, w_down[expert_id], preferred_element_type=jnp.float32).astype(jnp.bfloat16)
        pair_weight = flat_weight[pair_index]
        accum_out = accum_out.at[token_index].add(pair_weight[:, None] * expert_out.astype(jnp.float32), mode='drop')
        return (accum_out, None)
    accum_out, unused = lax.scan(expert_step, jnp.zeros((TOKENS, D), jnp.float32), jnp.arange(EXPERTS, dtype=jnp.int32))
    return (state_float + accum_out).astype(jnp.bfloat16)
```

```python
import math

import jax
import jax.numpy as jnp
from jax import lax
from jax.sharding import PartitionSpec as P

HD = 128


negative_fill = -1e30


def ring_order(count):
    return list(range(0, count, 2)) + list(range(count - 1, 0, -2))


def attend(queries, new_keys, new_values, cache_keys, cache_values, cache_len, span_req):
    spans = cache_keys.shape[0]
    cache_size = cache_keys.shape[1]
    length = queries.shape[0] // spans
    kv_local = cache_keys.shape[2] // HD
    head_count = queries.shape[1] // HD
    group_size = head_count // kv_local
    local_req = span_req % spans
    lengths = cache_len[local_req]
    queries_split = queries.reshape(spans, length, kv_local, group_size, HD)
    own_keys = new_keys.reshape(spans, length, kv_local, HD)
    own_values = new_values.reshape(spans, length, kv_local, HD)
    keys_cached = cache_keys[local_req].reshape(spans, cache_size, kv_local, HD)
    values_cached = cache_values[local_req].reshape(spans, cache_size, kv_local, HD)
    all_keys = jnp.concatenate([keys_cached, own_keys], axis=1)
    all_values = jnp.concatenate([values_cached, own_values], axis=1)
    scores = jnp.einsum(
        "clgqd,ckgd->cgqlk", queries_split, all_keys, preferred_element_type=jnp.float32
    ) * (1.0 / math.sqrt(HD))
    key_pos = jnp.arange(cache_size + length, dtype=jnp.int32)
    query_pos = jnp.arange(length, dtype=jnp.int32)
    in_cache = key_pos[None, None, :] < lengths[:, None, None]
    own_seen = key_pos[None, None, :] - cache_size <= query_pos[None, :, None]
    visible = jnp.where(key_pos[None, None, :] < cache_size, in_cache, own_seen)
    scores = jnp.where(visible[:, None, None], scores, negative_fill)
    weights = jax.nn.softmax(scores, axis=-1).astype(jnp.bfloat16)
    attended = jnp.einsum(
        "cgqlk,ckgd->clgqd", weights, all_values, preferred_element_type=jnp.float32
    )
    return attended.astype(jnp.bfloat16).reshape(spans * length, head_count * HD)


def routed_mix(normed, routes, gates, w_gate, w_up, w_down, capacity, experts):
    own_rows, model_width = normed.shape
    top_count = routes.shape[1]
    flat_routes = routes.reshape(-1)
    one_hot = (flat_routes[:, None] == jnp.arange(experts, dtype=jnp.int32)[None, :]).astype(
        jnp.int32
    )
    earlier = jnp.cumsum(one_hot, axis=0) - one_hot
    slot_index = jnp.sum(earlier * one_hot, axis=1)
    slot_target = flat_routes * capacity + slot_index
    pair_token = jnp.arange(flat_routes.shape[0], dtype=jnp.int32) // top_count
    source_row = (
        jnp.full((experts * capacity,), own_rows, jnp.int32).at[slot_target].set(pair_token)
    )
    padded_rows = jnp.concatenate([normed, jnp.zeros((1, model_width), jnp.bfloat16)], axis=0)
    outgoing = padded_rows[source_row].reshape(experts, capacity, model_width)
    slot_block = lax.all_to_all(
        outgoing, ("expert", "attn"), split_axis=0, concat_axis=0, tiled=True
    )
    rows_in = slot_block.reshape(-1, model_width)
    gate_part = jnp.dot(rows_in, w_gate[0], preferred_element_type=jnp.float32)
    up_part = jnp.dot(rows_in, w_up[0], preferred_element_type=jnp.float32)
    act = (jax.nn.silu(gate_part) * up_part).astype(jnp.bfloat16)
    expert_out = jnp.dot(act, w_down[0], preferred_element_type=jnp.float32).astype(jnp.bfloat16)
    computed = expert_out.reshape(slot_block.shape)
    returned = lax.all_to_all(computed, ("expert", "attn"), split_axis=0, concat_axis=0, tiled=True)
    picked = returned.reshape(experts * capacity, model_width)[slot_target].astype(jnp.float32)
    weight = gates / jnp.sum(gates, axis=-1, keepdims=True)
    return jnp.sum(
        (picked * weight.reshape(-1, 1)).reshape(own_rows, top_count, model_width), axis=1
    )


def ring_mix(normed, table, weights, n_expert):
    order = ring_order(n_expert)
    up = [(order[i], order[(i + 1) % n_expert]) for i in range(n_expert)]
    down = [(b, a) for a, b in up]
    place = jnp.zeros((n_expert,), jnp.int32).at[jnp.array(order)].set(jnp.arange(n_expert))
    order_of = jnp.array(order, jnp.int32)
    e = lax.axis_index("expert")
    c = lax.axis_index("attn")
    mine = place[e]
    rows = normed.shape[0]
    half = rows // 2
    tables = table.T[None]
    for bit in range(n_expert.bit_length() - 1):
        swap = [(i, i ^ (1 << bit)) for i in range(n_expert)]
        tables = jnp.concatenate([tables, lax.ppermute(tables, "expert", swap)], axis=0)
    (g0, u0, d0), (g1, u1, d1) = weights

    def column(source, expert):
        return lax.dynamic_slice(tables, (source ^ e, expert, 0), (1, 1, rows)).reshape(rows, 1)

    def contribution(block, source, lo, hi):
        out = None
        for g, u, d, expert in ((g0, u0, d0, 2 * e + c), (g1, u1, d1, 2 * e + 1 - c)):
            scale = column(source, expert)[lo:hi]
            gate_part = jnp.dot(block, g, preferred_element_type=jnp.float32)
            up_part = jnp.dot(block, u, preferred_element_type=jnp.float32)
            act = (jax.nn.silu(gate_part) * up_part * scale).astype(jnp.bfloat16)
            part = jnp.dot(act, d, preferred_element_type=jnp.float32)
            out = part if out is None else out + part
        return lax.optimization_barrier(out)

    reach = n_expert // 2
    ahead = behind = normed
    parts_up, parts_down = {}, {}
    home = contribution(normed, e, 0, rows)
    for step in range(1, reach + 1):
        if step < reach:
            ahead = lax.ppermute(ahead, "expert", up)
            behind = lax.ppermute(behind, "expert", down)
            src_a = order_of[(mine - step) % n_expert]
            src_b = order_of[(mine + step) % n_expert]
            parts_down[step] = contribution(ahead, src_a, 0, rows)
            parts_up[step] = contribution(behind, src_b, 0, rows)
        else:
            ahead = lax.ppermute(ahead[:half], "expert", up)
            behind = lax.ppermute(behind[half:], "expert", down)
            src = order_of[(mine + reach) % n_expert]
            both = contribution(jnp.concatenate([ahead, behind], axis=0), src, 0, rows)
            parts_up[step] = both[:half]
            parts_down[step] = both[half:]
    got_up = lax.ppermute(parts_up[reach].astype(jnp.bfloat16), "expert", up)
    got_down = lax.ppermute(parts_down[reach].astype(jnp.bfloat16), "expert", down)
    for step in range(reach - 1, 0, -1):
        if step == reach - 1:
            p = parts_up[step]
            send_up = jnp.concatenate([p[:half] + got_up.astype(jnp.float32), p[half:]], axis=0)
            q = parts_down[step]
            send_down = jnp.concatenate([q[:half], q[half:] + got_down.astype(jnp.float32)], axis=0)
        else:
            send_up = parts_up[step] + got_up.astype(jnp.float32)
            send_down = parts_down[step] + got_down.astype(jnp.float32)
        got_up = lax.ppermute(send_up.astype(jnp.bfloat16), "expert", up)
        got_down = lax.ppermute(send_down.astype(jnp.bfloat16), "expert", down)
    return home + got_up.astype(jnp.float32) + got_down.astype(jnp.float32)


def per_device(
    queries,
    new_keys,
    new_values,
    cache_keys,
    cache_values,
    cache_len,
    span_req,
    out_proj,
    resid,
    norm_gain,
    routes,
    gates,
    w_gate,
    w_up,
    w_down,
):
    n_attn = lax.axis_size("attn")
    n_expert = lax.axis_size("expert")
    own_rows = resid.shape[0]
    top_count = routes.shape[1]
    experts = n_expert * n_attn
    capacity = min(own_rows, 2 * top_count * own_rows // experts)
    dense = capacity == own_rows and n_attn == 2 and n_expert > 2 and n_expert & (n_expert - 1) == 0
    swap = [(0, 1), (1, 0)]
    if dense:
        mine = (w_gate[0], w_up[0], w_down[0])
        other = tuple(lax.ppermute(w, "attn", swap) for w in mine)
    attended = attend(
        queries, new_keys, new_values, cache_keys, cache_values, cache_len, span_req
    )
    if dense:
        c = lax.axis_index("attn")
        near = lax.dynamic_slice_in_dim(attended, c * own_rows, own_rows, 0)
        far = lax.dynamic_slice_in_dim(attended, (1 - c) * own_rows, own_rows, 0)
        theirs = jnp.dot(far, out_proj, preferred_element_type=jnp.float32)
        theirs = lax.ppermute(theirs, "attn", swap)
        attn_out = jnp.dot(near, out_proj, preferred_element_type=jnp.float32) + theirs
    else:
        attn_out = lax.psum_scatter(
            jnp.dot(attended, out_proj, preferred_element_type=jnp.float32),
            "attn",
            scatter_dimension=0,
            tiled=True,
        )
    hidden = (resid.astype(jnp.float32) + attn_out).astype(jnp.bfloat16)
    state_float = hidden.astype(jnp.float32)
    mean_square = jnp.mean(state_float * state_float, axis=-1, keepdims=True)
    normed = (state_float * lax.rsqrt(mean_square + 1e-06) * norm_gain).astype(jnp.bfloat16)
    if dense:
        weight = gates / jnp.sum(gates, axis=-1, keepdims=True)
        names = jnp.arange(experts, dtype=jnp.int32)
        table = jnp.sum(
            jnp.where(routes[:, :, None] == names[None, None, :], weight[:, :, None], 0.0), axis=1
        )
        mixed = ring_mix(normed, table, (mine, other), n_expert)
    else:
        mixed = routed_mix(normed, routes, gates, w_gate, w_up, w_down, capacity, experts)
    return (state_float + mixed).astype(jnp.bfloat16)


def solution(mesh):
    placed = (
        P(("groups", "expert"), "attn"),
        P(("groups", "expert"), "attn"),
        P(("groups", "expert"), "attn"),
        P(("groups", "expert"), None, "attn"),
        P(("groups", "expert"), None, "attn"),
        P(("groups", "expert")),
        P(("groups", "expert")),
        P("attn", None),
        P(("groups", "expert", "attn"), None),
        P(),
        P(("groups", "expert", "attn"), None),
        P(("groups", "expert", "attn"), None),
        P(("expert", "attn"), None, None),
        P(("expert", "attn"), None, None),
        P(("expert", "attn"), None, None),
    )
    return jax.shard_map(
        per_device,
        mesh=mesh,
        in_specs=placed,
        out_specs=P(("groups", "expert", "attn"), None),
        check_vma=False,
    )
```

```python
import functools
import math

import jax
import jax.numpy as jnp
from jax import lax
from jax.experimental import pallas as pl
from jax.experimental.pallas import tpu as pltpu
from jax.sharding import PartitionSpec as P


HD = 128
CHUNKS = 2
SMALL = pltpu.CompilerParams(vmem_limit_bytes=6 << 20)
VMEM = pl.BlockSpec(memory_space=pltpu.VMEM)
SMEM = pl.BlockSpec(memory_space=pltpu.SMEM)

negative_fill = -1e30


def ring_order(count):
    return list(range(0, count, 2)) + list(range(count - 1, 0, -2))


def place_of(chip, count):
    return jnp.where((chip & 1) == 0, chip >> 1, count - 1 - (chip >> 1))


def chip_at(place, count):
    return jnp.where(place < count // 2, 2 * place, 2 * (count - 1 - place) + 1)


def in_hbm(x):
    return pltpu.with_memory_space_constraint(x, pltpu.HBM)


def in_vmem(x):
    return pltpu.with_memory_space_constraint(x, pltpu.VMEM)


def attend_kernel(
    first_row,
    core,
    span_req,
    cache_len,
    q_ref,
    nk_ref,
    nv_ref,
    ck_ref,
    cv_ref,
    w_hbm,
    far_ref,
    near_ref,
    w_ref,
    w_sem,
):
    step = pl.program_id(0)
    spans = pl.num_programs(0)
    fetch = pltpu.make_async_copy(w_hbm, w_ref, w_sem)

    @pl.when(step == 0)
    def _():
        fetch.start()

    rows = q_ref.shape[0]
    heads = q_ref.shape[1] // HD
    length = nk_ref.shape[0]
    to_exp2 = math.log2(math.e) / math.sqrt(HD)
    span = lax.rem(core[0] + step + 1, spans)
    held = cache_len[lax.rem(span_req[span], spans)]
    q = jnp.concatenate([q_ref[:, h * HD : (h + 1) * HD] for h in range(heads)], axis=0)
    dims = (((1,), (1,)), ((), ()))
    old = lax.dot_general(q, ck_ref[0], dims, preferred_element_type=jnp.float32)
    new = lax.dot_general(q, nk_ref[...], dims, preferred_element_type=jnp.float32)
    key_at = lax.broadcasted_iota(jnp.int32, (1, old.shape[1]), 1)
    old = jnp.where(key_at < held, old, negative_fill)
    own_at = lax.broadcasted_iota(jnp.int32, (rows, length), 1)
    own_row = first_row + lax.broadcasted_iota(jnp.int32, (rows, length), 0)
    fill = jnp.where(own_at <= own_row, 0.0, negative_fill)
    new = new + jnp.concatenate([fill] * heads, axis=0)
    top = jnp.maximum(
        jnp.max(old, axis=1, keepdims=True), jnp.max(new, axis=1, keepdims=True)
    )
    old = jnp.exp2((old - top) * to_exp2)
    new = jnp.exp2((new - top) * to_exp2)
    total = jnp.sum(old, axis=1, keepdims=True) + jnp.sum(new, axis=1, keepdims=True)
    out = jnp.dot(old.astype(jnp.bfloat16), cv_ref[0], preferred_element_type=jnp.float32)
    out += jnp.dot(new.astype(jnp.bfloat16), nv_ref[...], preferred_element_type=jnp.float32)
    out = (out / total).astype(jnp.bfloat16)
    out = jnp.concatenate([out[h * rows : (h + 1) * rows] for h in range(heads)], axis=1)

    @pl.when(step == 0)
    def _():
        fetch.wait()

    out = jnp.dot(out, w_ref[...], preferred_element_type=jnp.float32)

    @pl.when(step == 0)
    def _():
        far_ref[...] = out

    @pl.when(step == spans - 1)
    def _():
        near_ref[...] = out


def attend_chunk(
    chunk,
    core,
    span_req,
    cache_len,
    queries,
    new_keys,
    new_values,
    cache_keys,
    cache_values,
    out_proj,
):
    spans, cache_size, _ = cache_keys.shape
    length = queries.shape[0] // spans
    rows = length // CHUNKS
    width = out_proj.shape[1]
    shape = pltpu.VMEM((rows, width), jnp.float32)
    macs = spans * rows * (queries.shape[1] * (2 * (cache_size + length) + width))

    def span_at(i, core):
        return lax.rem(core[0] + i + 1, spans)

    def request_at(i, core, span_req):
        return lax.rem(span_req[span_at(i, core)], spans)

    new_spec = pl.BlockSpec((length, HD), lambda i, c, r, n: (span_at(i, c), 0))
    old_spec = pl.BlockSpec((1, cache_size, HD), lambda i, c, r, n: (request_at(i, c, r), 0, 0))
    out_spec = pl.BlockSpec((rows, width), lambda i, c, r, n: (0, 0))
    return pl.pallas_call(
        functools.partial(attend_kernel, chunk * rows),
        out_shape=(shape, shape),
        grid_spec=pltpu.PrefetchScalarGridSpec(
            num_scalar_prefetch=3,
            grid=(spans,),
            in_specs=[
                pl.BlockSpec(
                    (rows, queries.shape[1]),
                    lambda i, c, r, n: (span_at(i, c) * CHUNKS + chunk, 0),
                ),
                new_spec,
                new_spec,
                old_spec,
                old_spec,
                pl.BlockSpec(memory_space=pltpu.HBM),
            ],
            out_specs=[out_spec, out_spec],
            scratch_shapes=[
                pltpu.VMEM(out_proj.shape, out_proj.dtype),
                pltpu.SemaphoreType.DMA,
            ],
        ),
        cost_estimate=pl.CostEstimate(
            flops=2 * macs, transcendentals=0, bytes_accessed=out_proj.size * 2
        ),
        compiler_params=pltpu.CompilerParams(vmem_limit_bytes=20 << 20),
        name="attend",
    )(
        core,
        span_req,
        cache_len,
        *map(in_hbm, (queries, new_keys, new_values, cache_keys, cache_values, out_proj)),
    )


def norm_kernel(near_ref, far_ref, resid_ref, gain_ref, hidden_ref, normed_ref):
    state = resid_ref[...].astype(jnp.float32) + (near_ref[...] + far_ref[...])
    state = state.astype(jnp.bfloat16)
    hidden_ref[...] = state
    state = state.astype(jnp.float32)
    mean_square = jnp.mean(state * state, axis=-1, keepdims=True)
    normed_ref[...] = (state * lax.rsqrt(mean_square + 1e-06) * gain_ref[...]).astype(jnp.bfloat16)


def norm_chunk(chunk, near, far, resid, gain):
    rows, width = near.shape
    whole = pl.BlockSpec((rows, width), lambda i: (0, 0))
    return pl.pallas_call(
        norm_kernel,
        grid=(1,),
        out_shape=(pltpu.VMEM((rows, width), jnp.bfloat16),) * 2,
        in_specs=[
            whole,
            whole,
            pl.BlockSpec((rows, width), lambda i: (chunk, 0)),
            pl.BlockSpec((1, width), lambda i: (0, 0)),
        ],
        out_specs=(whole, whole),
        compiler_params=SMALL,
        name="norm",
    )(in_vmem(near), in_vmem(far), in_hbm(resid), gain.reshape(1, width))


def experts_kernel(n_expert, firsts, offsets, ids, *refs):
    count = len(firsts)
    e, c = ids[0], ids[1]
    at = place_of(e, n_expert)
    local = (2 * e + c, 2 * e + 1 - c)
    blocks, (tables_ref, g0, u0, d0, g1, u1, d1), outs = (
        refs[:count],
        refs[count : count + 7],
        refs[count + 7 :],
    )
    rows = blocks[0].shape[0]
    x = jnp.concatenate([b[...] for b in blocks], axis=0) if count > 1 else blocks[0][...]
    turned = [
        jnp.transpose(tables_ref[chip_at(lax.rem(at + o + n_expert, n_expert), n_expert) ^ e])
        for o in offsets
    ]
    name_at = lax.broadcasted_iota(jnp.int32, turned[0].shape, 1)
    total = None
    for j, (g, u, d) in enumerate(((g0, u0, d0), (g1, u1, d1))):
        scale = jnp.concatenate(
            [
                jnp.sum(jnp.where(name_at == local[j], t, 0.0), axis=1, keepdims=True)[f : f + rows]
                for t, f in zip(turned, firsts)
            ],
            axis=0,
        )
        gate_part = jnp.dot(x, g[...], preferred_element_type=jnp.float32)
        up_part = jnp.dot(x, u[...], preferred_element_type=jnp.float32)
        act = gate_part / (1.0 + jnp.exp(-gate_part)) * up_part * scale
        part = jnp.dot(act.astype(jnp.bfloat16), d[...], preferred_element_type=jnp.float32)
        total = part if total is None else total + part
    for i, out in enumerate(outs):
        out[...] = total[i * rows : (i + 1) * rows].astype(out.dtype)


def run_experts(n_expert, ids, blocks, firsts, offsets, kinds, tables, mine, other):
    rows, width = blocks[0].shape
    weights = (*mine, *other)
    outs = tuple(pltpu.VMEM((rows, width), kind) for kind in kinds)
    flops = 2 * rows * len(blocks) * sum(w.size for w in weights)
    return pl.pallas_call(
        functools.partial(experts_kernel, n_expert, firsts, offsets),
        out_shape=outs,
        in_specs=[SMEM]
        + [VMEM] * (len(blocks) + 1 + len(weights)),
        out_specs=tuple(VMEM for _ in blocks),
        cost_estimate=pl.CostEstimate(
            flops=flops, transcendentals=0, bytes_accessed=sum(w.size for w in weights) * 2
        ),
        compiler_params=pltpu.CompilerParams(vmem_limit_bytes=12 << 20),
        name="experts",
    )(ids, *map(in_vmem, blocks), in_vmem(tables), *map(in_vmem, weights))


def add_kernel(count, *refs):
    for part, got, out in zip(refs[:count], refs[count : 2 * count], refs[2 * count :]):
        out[...] = (part[...] + got[...].astype(jnp.float32)).astype(out.dtype)


def add_parts(parts, arrived):
    count = len(parts)
    return pl.pallas_call(
        functools.partial(add_kernel, count),
        out_shape=tuple(pltpu.VMEM(x.shape, x.dtype) for x in arrived),
        in_specs=[VMEM] * (2 * count),
        out_specs=(VMEM,) * count,
        compiler_params=SMALL,
        name="add",
    )(*map(in_vmem, (*parts, *arrived)))


def final_kernel(count, *refs):
    out_ref = refs[-1]
    rows = refs[0].shape[0]
    for k in range(count):
        hidden, home, ahead, behind = (refs[i * count + k][...] for i in range(4))
        mixed = home + ahead.astype(jnp.float32) + behind.astype(jnp.float32)
        out_ref[k * rows : (k + 1) * rows] = (hidden.astype(jnp.float32) + mixed).astype(
            out_ref.dtype
        )


def finish(hidden, home, ahead, behind):
    count = len(hidden)
    rows, width = hidden[0].shape
    return pl.pallas_call(
        functools.partial(final_kernel, count),
        out_shape=jax.ShapeDtypeStruct((count * rows, width), jnp.bfloat16),
        in_specs=[VMEM] * (4 * count),
        out_specs=VMEM,
        compiler_params=SMALL,
        name="finish",
    )(*map(in_vmem, (*hidden, *home, *ahead, *behind)))


def weigh_kernel(routes_ref, gates_ref, out_ref):
    gates = gates_ref[...]
    weight = gates / jnp.sum(gates, axis=0, keepdims=True)
    routes = routes_ref[...]
    out_ref[0] = jnp.concatenate(
        [
            jnp.sum(jnp.where(routes == j, weight, 0.0), axis=0, keepdims=True)
            for j in range(out_ref.shape[1])
        ],
        axis=0,
    )


def weigh(routes, gates, experts):
    return pl.pallas_call(
        weigh_kernel,
        out_shape=pltpu.VMEM((1, experts, routes.shape[0]), jnp.float32),
        in_specs=[VMEM] * 2,
        out_specs=VMEM,
        compiler_params=SMALL,
        name="weigh",
    )(routes.T, gates.T)


def dense_layer(
    queries,
    new_keys,
    new_values,
    cache_keys,
    cache_values,
    cache_len,
    span_req,
    out_proj,
    resid,
    norm_gain,
    routes,
    gates,
    w_gate,
    w_up,
    w_down,
):
    n_expert = lax.axis_size("expert")
    experts = n_expert * lax.axis_size("attn")
    e = lax.axis_index("expert")
    c = lax.axis_index("attn")
    own_rows = resid.shape[0]
    rows = own_rows // CHUNKS
    swap = [(0, 1), (1, 0)]
    order = ring_order(n_expert)
    steps = {}
    steps[1] = [(order[i], order[(i + 1) % n_expert]) for i in range(n_expert)]
    steps[-1] = [(b, a) for a, b in steps[1]]
    reach = n_expert // 2

    mine = (w_gate[0], w_up[0], w_down[0])
    other = tuple(lax.ppermute(w, "attn", swap) for w in mine)

    tables = weigh(routes, gates, experts)
    for bit in range(n_expert.bit_length() - 1):
        pairs = [(i, i ^ (1 << bit)) for i in range(n_expert)]
        tables = jnp.concatenate([tables, lax.ppermute(tables, "expert", pairs)], axis=0)

    core = c.reshape(1)
    ids = jnp.stack([e, c])
    near, far = [], []
    for k in range(CHUNKS):
        theirs, ours = attend_chunk(
            k,
            core,
            span_req,
            cache_len,
            queries,
            new_keys,
            new_values,
            cache_keys,
            cache_values,
            out_proj,
        )
        near.append(ours)
        far.append(lax.ppermute(theirs, "attn", swap))
    hidden, normed = [], []
    for k in range(CHUNKS):
        h, x = norm_chunk(k, near[k], far[k], resid, norm_gain)
        hidden.append(h)
        normed.append(x)

    def compute(blocks, firsts, offsets, kinds):
        return run_experts(
            n_expert, ids, blocks, firsts, offsets, kinds, tables, mine, other
        )

    wide, sent = jnp.float32, jnp.bfloat16
    longer = [1 if k % 2 == 0 else -1 for k in range(CHUNKS)]
    shorter = [-way for way in longer]
    parts = [{} for _ in range(CHUNKS)]
    moving = [{1: x, -1: x} for x in normed]
    home = compute(normed, [k * rows for k in range(CHUNKS)], [0] * CHUNKS, [wide] * CHUNKS)
    for s in range(1, reach):
        for k in range(CHUNKS):
            for way in (1, -1):
                moving[k][way] = lax.ppermute(moving[k][way], "expert", steps[way])
            got = compute(
                [moving[k][way] for way in (1, -1)],
                [k * rows] * 2,
                [-s, s],
                [sent if o == shorter[k] * (reach - 1) else wide for o in (-s, s)],
            )
            parts[k][-s], parts[k][s] = got
    last = []
    for k in range(CHUNKS):
        last.append(lax.ppermute(moving[k][longer[k]], "expert", steps[longer[k]]))
    got = compute(last, [k * rows for k in range(CHUNKS)], [reach] * CHUNKS, [sent] * CHUNKS)

    def send(blocks, ways):
        return [lax.ppermute(x, "expert", steps[way]) for x, way in zip(blocks, ways)]

    early = [(parts[k][shorter[k] * (reach - 1)]) for k in range(CHUNKS)]
    early = send(early, shorter)
    late = send(got, longer)
    for s in range(reach - 1, 0, -1):
        late = add_parts([parts[k][longer[k] * s] for k in range(CHUNKS)], late)
        late = send(late, longer)
        if s > 1:
            early = add_parts([parts[k][shorter[k] * (s - 1)] for k in range(CHUNKS)], early)
            early = send(early, shorter)
    return finish(hidden, home, early, late)


def attend(queries, new_keys, new_values, cache_keys, cache_values, cache_len, span_req):
    spans = cache_keys.shape[0]
    cache_size = cache_keys.shape[1]
    length = queries.shape[0] // spans
    kv_local = cache_keys.shape[2] // HD
    head_count = queries.shape[1] // HD
    group_size = head_count // kv_local
    local_req = span_req % spans
    lengths = cache_len[local_req]
    queries_split = queries.reshape(spans, length, kv_local, group_size, HD)
    own_keys = new_keys.reshape(spans, length, kv_local, HD)
    own_values = new_values.reshape(spans, length, kv_local, HD)
    keys_cached = cache_keys[local_req].reshape(spans, cache_size, kv_local, HD)
    values_cached = cache_values[local_req].reshape(spans, cache_size, kv_local, HD)
    all_keys = jnp.concatenate([keys_cached, own_keys], axis=1)
    all_values = jnp.concatenate([values_cached, own_values], axis=1)
    scores = jnp.einsum(
        "clgqd,ckgd->cgqlk", queries_split, all_keys, preferred_element_type=jnp.float32
    ) * (1.0 / math.sqrt(HD))
    key_pos = jnp.arange(cache_size + length, dtype=jnp.int32)
    query_pos = jnp.arange(length, dtype=jnp.int32)
    in_cache = key_pos[None, None, :] < lengths[:, None, None]
    own_seen = key_pos[None, None, :] - cache_size <= query_pos[None, :, None]
    visible = jnp.where(key_pos[None, None, :] < cache_size, in_cache, own_seen)
    scores = jnp.where(visible[:, None, None], scores, negative_fill)
    weights = jax.nn.softmax(scores, axis=-1).astype(jnp.bfloat16)
    attended = jnp.einsum(
        "cgqlk,ckgd->clgqd", weights, all_values, preferred_element_type=jnp.float32
    )
    return attended.astype(jnp.bfloat16).reshape(spans * length, head_count * HD)


def routed_mix(normed, routes, gates, w_gate, w_up, w_down, capacity, experts):
    own_rows, model_width = normed.shape
    top_count = routes.shape[1]
    flat_routes = routes.reshape(-1)
    one_hot = (flat_routes[:, None] == jnp.arange(experts, dtype=jnp.int32)[None, :]).astype(
        jnp.int32
    )
    earlier = jnp.cumsum(one_hot, axis=0) - one_hot
    slot_index = jnp.sum(earlier * one_hot, axis=1)
    slot_target = flat_routes * capacity + slot_index
    pair_token = jnp.arange(flat_routes.shape[0], dtype=jnp.int32) // top_count
    source_row = (
        jnp.full((experts * capacity,), own_rows, jnp.int32).at[slot_target].set(pair_token)
    )
    padded_rows = jnp.concatenate([normed, jnp.zeros((1, model_width), jnp.bfloat16)], axis=0)
    outgoing = padded_rows[source_row].reshape(experts, capacity, model_width)
    slot_block = lax.all_to_all(
        outgoing, ("expert", "attn"), split_axis=0, concat_axis=0, tiled=True
    )
    rows_in = slot_block.reshape(-1, model_width)
    gate_part = jnp.dot(rows_in, w_gate[0], preferred_element_type=jnp.float32)
    up_part = jnp.dot(rows_in, w_up[0], preferred_element_type=jnp.float32)
    act = (jax.nn.silu(gate_part) * up_part).astype(jnp.bfloat16)
    expert_out = jnp.dot(act, w_down[0], preferred_element_type=jnp.float32).astype(jnp.bfloat16)
    computed = expert_out.reshape(slot_block.shape)
    returned = lax.all_to_all(computed, ("expert", "attn"), split_axis=0, concat_axis=0, tiled=True)
    picked = returned.reshape(experts * capacity, model_width)[slot_target].astype(jnp.float32)
    weight = gates / jnp.sum(gates, axis=-1, keepdims=True)
    return jnp.sum(
        (picked * weight.reshape(-1, 1)).reshape(own_rows, top_count, model_width), axis=1
    )


def routed_layer(
    queries,
    new_keys,
    new_values,
    cache_keys,
    cache_values,
    cache_len,
    span_req,
    out_proj,
    resid,
    norm_gain,
    routes,
    gates,
    w_gate,
    w_up,
    w_down,
):
    experts = lax.axis_size("expert") * lax.axis_size("attn")
    capacity = 2 * routes.shape[1] * resid.shape[0] // experts
    attended = attend(
        queries, new_keys, new_values, cache_keys, cache_values, cache_len, span_req
    )
    attn_out = lax.psum_scatter(
        jnp.dot(attended, out_proj, preferred_element_type=jnp.float32),
        "attn",
        scatter_dimension=0,
        tiled=True,
    )
    hidden = (resid.astype(jnp.float32) + attn_out).astype(jnp.bfloat16)
    state_float = hidden.astype(jnp.float32)
    mean_square = jnp.mean(state_float * state_float, axis=-1, keepdims=True)
    normed = (state_float * lax.rsqrt(mean_square + 1e-06) * norm_gain).astype(jnp.bfloat16)
    mixed = routed_mix(normed, routes, gates, w_gate, w_up, w_down, capacity, experts)
    return (state_float + mixed).astype(jnp.bfloat16)


def per_device(*args):
    cache_keys, routes = args[3], args[10]
    n_expert, n_attn = lax.axis_size("expert"), lax.axis_size("attn")
    everywhere = 2 * routes.shape[1] >= n_expert * n_attn
    fits = n_attn == 2 and n_expert > 2 and n_expert & (n_expert - 1) == 0
    fits = fits and cache_keys.shape[0] == 2 and cache_keys.shape[2] == HD
    if everywhere and fits:
        return dense_layer(*args)
    return routed_layer(*args)


def solution(mesh):
    placed = (
        P(("groups", "expert"), "attn"),
        P(("groups", "expert"), "attn"),
        P(("groups", "expert"), "attn"),
        P(("groups", "expert"), None, "attn"),
        P(("groups", "expert"), None, "attn"),
        P(("groups", "expert")),
        P(("groups", "expert")),
        P("attn", None),
        P(("groups", "expert", "attn"), None),
        P(),
        P(("groups", "expert", "attn"), None),
        P(("groups", "expert", "attn"), None),
        P(("expert", "attn"), None, None),
        P(("expert", "attn"), None, None),
        P(("expert", "attn"), None, None),
    )
    return jax.shard_map(
        per_device,
        mesh=mesh,
        in_specs=placed,
        out_specs=P(("groups", "expert", "attn"), None),
        check_vma=False,
    )
```

```python
import functools
import math

import jax
import jax.numpy as jnp
from jax import lax
from jax.experimental import pallas as pl
from jax.experimental.pallas import tpu as pltpu
from jax.sharding import PartitionSpec as P


HD = 128
CHUNKS = 2
SMALL = pltpu.CompilerParams(vmem_limit_bytes=6 << 20)
VMEM = pl.BlockSpec(memory_space=pltpu.VMEM)
SMEM = pl.BlockSpec(memory_space=pltpu.SMEM)

negative_fill = -1e30


def ring_order(count):
    return list(range(0, count, 2)) + list(range(count - 1, 0, -2))


def place_of(chip, count):
    return jnp.where((chip & 1) == 0, chip >> 1, count - 1 - (chip >> 1))


def chip_at(place, count):
    return jnp.where(place < count // 2, 2 * place, 2 * (count - 1 - place) + 1)


def in_hbm(x):
    return pltpu.with_memory_space_constraint(x, pltpu.HBM)


def in_vmem(x):
    return pltpu.with_memory_space_constraint(x, pltpu.VMEM)


def attend_kernel(
    first_row,
    ids,
    span_req,
    cache_len,
    q_hbm,
    nk_hbm,
    nv_hbm,
    ck_hbm,
    cv_hbm,
    w_hbm,
    far_ref,
    near_ref,
    q_ref,
    nk_ref,
    nv_ref,
    ck_ref,
    cv_ref,
    w_ref,
    sems,
):
    spans, rows, width = q_ref.shape
    heads = width // HD
    length = nk_ref.shape[1]
    to_exp2 = math.log2(math.e) / math.sqrt(HD)
    dims = (((1,), (1,)), ((), ()))
    copies, held = [], []
    for i in range(spans):
        span = lax.rem(ids[1] + i + 1, spans)
        request = lax.rem(span_req[span], spans)
        held.append(cache_len[request])
        first = pl.multiple_of(span * length, length)
        sources = (
            q_hbm.at[pl.ds(pl.multiple_of(first + first_row, rows), rows)],
            ck_hbm.at[request],
            nk_hbm.at[pl.ds(first, length)],
            cv_hbm.at[request],
            nv_hbm.at[pl.ds(first, length)],
        )
        copies.append(
            [
                pltpu.make_async_copy(source, target.at[i], sems.at[i, j])
                for j, (source, target) in enumerate(
                    zip(sources, (q_ref, ck_ref, nk_ref, cv_ref, nv_ref))
                )
            ]
        )
        for copy in copies[i]:
            copy.start()
    fetch = pltpu.make_async_copy(w_hbm, w_ref, sems.at[spans, 0])
    fetch.start()
    own_at = lax.broadcasted_iota(jnp.int32, (rows, length), 1)
    own_row = first_row + lax.broadcasted_iota(jnp.int32, (rows, length), 0)
    fill = jnp.where(own_at <= own_row, 0.0, negative_fill)
    fill = jnp.concatenate([fill] * heads, axis=0)
    key_at = lax.broadcasted_iota(jnp.int32, (1, ck_ref.shape[1]), 1)
    attended = []
    for i in range(spans):
        for copy in copies[i][:3]:
            copy.wait()
        q = jnp.concatenate([q_ref[i, :, h * HD : (h + 1) * HD] for h in range(heads)], axis=0)
        old = lax.dot_general(q, ck_ref[i], dims, preferred_element_type=jnp.float32)
        new = lax.dot_general(q, nk_ref[i], dims, preferred_element_type=jnp.float32) + fill
        old = jnp.where(key_at < held[i], old, negative_fill)
        top = jnp.maximum(
            jnp.max(old, axis=1, keepdims=True), jnp.max(new, axis=1, keepdims=True)
        )
        old = jnp.exp2((old - top) * to_exp2)
        new = jnp.exp2((new - top) * to_exp2)
        total = jnp.sum(old, axis=1, keepdims=True) + jnp.sum(new, axis=1, keepdims=True)
        for copy in copies[i][3:]:
            copy.wait()
        out = jnp.dot(old.astype(jnp.bfloat16), cv_ref[i], preferred_element_type=jnp.float32)
        out += jnp.dot(new.astype(jnp.bfloat16), nv_ref[i], preferred_element_type=jnp.float32)
        out = (out / total).astype(jnp.bfloat16)
        attended.append(
            jnp.concatenate([out[h * rows : (h + 1) * rows] for h in range(heads)], axis=1)
        )
    fetch.wait()
    out = jnp.dot(
        jnp.concatenate(attended, axis=0), w_ref[...], preferred_element_type=jnp.float32
    )
    far_ref[...] = out[:rows]
    near_ref[...] = out[rows:]


def attend_chunk(
    chunk,
    ids,
    span_req,
    cache_len,
    queries,
    new_keys,
    new_values,
    cache_keys,
    cache_values,
    out_proj,
):
    spans, cache_size, _ = cache_keys.shape
    length = queries.shape[0] // spans
    rows = length // CHUNKS
    width = out_proj.shape[1]
    kind = queries.dtype
    macs = spans * rows * (queries.shape[1] * (2 * (cache_size + length) + width))
    return pl.pallas_call(
        functools.partial(attend_kernel, chunk * rows),
        out_shape=(pltpu.VMEM((rows, width), jnp.float32),) * 2,
        in_specs=[SMEM] * 3 + [pl.BlockSpec(memory_space=pltpu.HBM)] * 6,
        out_specs=(VMEM,) * 2,
        scratch_shapes=[
            pltpu.VMEM((spans, rows, queries.shape[1]), kind),
            pltpu.VMEM((spans, length, HD), kind),
            pltpu.VMEM((spans, length, HD), kind),
            pltpu.VMEM(cache_keys.shape, kind),
            pltpu.VMEM(cache_keys.shape, kind),
            pltpu.VMEM(out_proj.shape, kind),
            pltpu.SemaphoreType.DMA((spans + 1, 5)),
        ],
        cost_estimate=pl.CostEstimate(
            flops=2 * macs, transcendentals=0, bytes_accessed=out_proj.size * 2
        ),
        compiler_params=pltpu.CompilerParams(vmem_limit_bytes=24 << 20),
        name="attend",
    )(
        ids,
        *map(in_hbm, (span_req, cache_len)),
        *map(in_hbm, (queries, new_keys, new_values, cache_keys, cache_values, out_proj)),
    )


def norm_kernel(first_row, near_ref, far_ref, resid_ref, gain_ref, hidden_ref, normed_ref):
    rows = near_ref.shape[0]
    state = resid_ref[first_row : first_row + rows].astype(jnp.float32)
    state = (state + (near_ref[...] + far_ref[...])).astype(jnp.bfloat16)
    hidden_ref[...] = state
    state = state.astype(jnp.float32)
    mean_square = jnp.mean(state * state, axis=-1, keepdims=True)
    normed_ref[...] = (state * lax.rsqrt(mean_square + 1e-06) * gain_ref[...]).astype(jnp.bfloat16)


def norm_chunk(chunk, near, far, resid, gain):
    rows, width = near.shape
    return pl.pallas_call(
        functools.partial(norm_kernel, chunk * rows),
        out_shape=(pltpu.VMEM((rows, width), jnp.bfloat16),) * 2,
        in_specs=[VMEM] * 4,
        out_specs=(VMEM,) * 2,
        compiler_params=SMALL,
        name="norm",
    )(*map(in_vmem, (near, far, resid, gain.reshape(1, width))))


def experts_kernel(n_expert, firsts, offsets, ids, *refs):
    count = len(firsts)
    e, c = ids[0], ids[1]
    at = place_of(e, n_expert)
    local = (2 * e + c, 2 * e + 1 - c)
    blocks, (tables_ref, g0, u0, d0, g1, u1, d1), outs = (
        refs[:count],
        refs[count : count + 7],
        refs[count + 7 :],
    )
    rows = blocks[0].shape[0]
    x = jnp.concatenate([b[...] for b in blocks], axis=0) if count > 1 else blocks[0][...]
    turned = [
        jnp.transpose(tables_ref[chip_at(lax.rem(at + o + n_expert, n_expert), n_expert) ^ e])
        for o in offsets
    ]
    name_at = lax.broadcasted_iota(jnp.int32, turned[0].shape, 1)
    total = None
    for j, (g, u, d) in enumerate(((g0, u0, d0), (g1, u1, d1))):
        scale = jnp.concatenate(
            [
                jnp.sum(jnp.where(name_at == local[j], t, 0.0), axis=1, keepdims=True)[f : f + rows]
                for t, f in zip(turned, firsts)
            ],
            axis=0,
        )
        gate_part = jnp.dot(x, g[...], preferred_element_type=jnp.float32)
        up_part = jnp.dot(x, u[...], preferred_element_type=jnp.float32)
        act = gate_part / (1.0 + jnp.exp(-gate_part)) * up_part * scale
        part = jnp.dot(act.astype(jnp.bfloat16), d[...], preferred_element_type=jnp.float32)
        total = part if total is None else total + part
    for i, out in enumerate(outs):
        out[...] = total[i * rows : (i + 1) * rows].astype(out.dtype)


def run_experts(n_expert, ids, blocks, firsts, offsets, kinds, tables, mine, other):
    rows, width = blocks[0].shape
    weights = (*mine, *other)
    outs = tuple(pltpu.VMEM((rows, width), kind) for kind in kinds)
    flops = 2 * rows * len(blocks) * sum(w.size for w in weights)
    return pl.pallas_call(
        functools.partial(experts_kernel, n_expert, firsts, offsets),
        out_shape=outs,
        in_specs=[SMEM]
        + [VMEM] * (len(blocks) + 1 + len(weights)),
        out_specs=tuple(VMEM for _ in blocks),
        cost_estimate=pl.CostEstimate(
            flops=flops, transcendentals=0, bytes_accessed=sum(w.size for w in weights) * 2
        ),
        compiler_params=pltpu.CompilerParams(vmem_limit_bytes=12 << 20),
        name="experts",
    )(ids, *map(in_vmem, blocks), in_vmem(tables), *map(in_vmem, weights))


def add_kernel(count, *refs):
    for part, got, out in zip(refs[:count], refs[count : 2 * count], refs[2 * count :]):
        out[...] = (part[...] + got[...].astype(jnp.float32)).astype(out.dtype)


def add_parts(parts, arrived):
    count = len(parts)
    return pl.pallas_call(
        functools.partial(add_kernel, count),
        out_shape=tuple(pltpu.VMEM(x.shape, x.dtype) for x in arrived),
        in_specs=[VMEM] * (2 * count),
        out_specs=(VMEM,) * count,
        compiler_params=SMALL,
        name="add",
    )(*map(in_vmem, (*parts, *arrived)))


def final_kernel(count, *refs):
    out_ref = refs[-1]
    rows = refs[0].shape[0]
    for k in range(count):
        hidden, home, ahead, behind = (refs[i * count + k][...] for i in range(4))
        mixed = home + ahead.astype(jnp.float32) + behind.astype(jnp.float32)
        out_ref[k * rows : (k + 1) * rows] = (hidden.astype(jnp.float32) + mixed).astype(
            out_ref.dtype
        )


def finish(hidden, home, ahead, behind):
    count = len(hidden)
    rows, width = hidden[0].shape
    return pl.pallas_call(
        functools.partial(final_kernel, count),
        out_shape=jax.ShapeDtypeStruct((count * rows, width), jnp.bfloat16),
        in_specs=[VMEM] * (4 * count),
        out_specs=VMEM,
        compiler_params=SMALL,
        name="finish",
    )(*map(in_vmem, (*hidden, *home, *ahead, *behind)))


def weigh_kernel(routes_ref, gates_ref, out_ref):
    gates = gates_ref[...]
    weight = gates / jnp.sum(gates, axis=0, keepdims=True)
    routes = routes_ref[...]
    out_ref[0] = jnp.concatenate(
        [
            jnp.sum(jnp.where(routes == j, weight, 0.0), axis=0, keepdims=True)
            for j in range(out_ref.shape[1])
        ],
        axis=0,
    )


def weigh(routes, gates, experts):
    return pl.pallas_call(
        weigh_kernel,
        out_shape=pltpu.VMEM((1, experts, routes.shape[0]), jnp.float32),
        in_specs=[VMEM] * 2,
        out_specs=VMEM,
        compiler_params=SMALL,
        name="weigh",
    )(routes.T, gates.T)


def dense_layer(
    queries,
    new_keys,
    new_values,
    cache_keys,
    cache_values,
    cache_len,
    span_req,
    out_proj,
    resid,
    norm_gain,
    routes,
    gates,
    w_gate,
    w_up,
    w_down,
):
    n_expert = lax.axis_size("expert")
    experts = n_expert * lax.axis_size("attn")
    e = lax.axis_index("expert")
    c = lax.axis_index("attn")
    own_rows = resid.shape[0]
    rows = own_rows // CHUNKS
    swap = [(0, 1), (1, 0)]
    order = ring_order(n_expert)
    steps = {}
    steps[1] = [(order[i], order[(i + 1) % n_expert]) for i in range(n_expert)]
    steps[-1] = [(b, a) for a, b in steps[1]]
    reach = n_expert // 2

    ids = jnp.stack([e, c])
    mine = (w_gate[0], w_up[0], w_down[0])
    other = tuple(lax.ppermute(w, "attn", swap) for w in mine)
    tables = weigh(routes, gates, experts)
    for bit in range(n_expert.bit_length() - 1):
        pairs = [(i, i ^ (1 << bit)) for i in range(n_expert)]
        tables = jnp.concatenate([tables, lax.ppermute(tables, "expert", pairs)], axis=0)

    near, far = [], []
    for k in range(CHUNKS):
        theirs, ours = attend_chunk(
            k,
            ids,
            span_req,
            cache_len,
            queries,
            new_keys,
            new_values,
            cache_keys,
            cache_values,
            out_proj,
        )
        near.append(ours)
        far.append(lax.ppermute(theirs, "attn", swap))
    hidden, normed = [], []
    for k in range(CHUNKS):
        h, x = norm_chunk(k, near[k], far[k], resid, norm_gain)
        hidden.append(h)
        normed.append(x)

    def compute(blocks, firsts, offsets, kinds):
        return run_experts(
            n_expert, ids, blocks, firsts, offsets, kinds, tables, mine, other
        )

    wide, sent = jnp.float32, jnp.bfloat16
    longer = [1 if k % 2 == 0 else -1 for k in range(CHUNKS)]
    shorter = [-way for way in longer]
    parts = [{} for _ in range(CHUNKS)]
    moving = [{1: x, -1: x} for x in normed]
    home = compute(normed, [k * rows for k in range(CHUNKS)], [0] * CHUNKS, [wide] * CHUNKS)
    for s in range(1, reach):
        for k in range(CHUNKS):
            for way in (1, -1):
                moving[k][way] = lax.ppermute(moving[k][way], "expert", steps[way])
            got = compute(
                [moving[k][way] for way in (1, -1)],
                [k * rows] * 2,
                [-s, s],
                [sent if o == shorter[k] * (reach - 1) else wide for o in (-s, s)],
            )
            parts[k][-s], parts[k][s] = got
    last = []
    for k in range(CHUNKS):
        last.append(lax.ppermute(moving[k][longer[k]], "expert", steps[longer[k]]))
    got = compute(last, [k * rows for k in range(CHUNKS)], [reach] * CHUNKS, [sent] * CHUNKS)

    def send(blocks, ways):
        return [lax.ppermute(x, "expert", steps[way]) for x, way in zip(blocks, ways)]

    early = [(parts[k][shorter[k] * (reach - 1)]) for k in range(CHUNKS)]
    early = send(early, shorter)
    late = send(got, longer)
    for s in range(reach - 1, 0, -1):
        late = add_parts([parts[k][longer[k] * s] for k in range(CHUNKS)], late)
        late = send(late, longer)
        if s > 1:
            early = add_parts([parts[k][shorter[k] * (s - 1)] for k in range(CHUNKS)], early)
            early = send(early, shorter)
    return finish(hidden, home, early, late)


def attend(queries, new_keys, new_values, cache_keys, cache_values, cache_len, span_req):
    spans = cache_keys.shape[0]
    cache_size = cache_keys.shape[1]
    length = queries.shape[0] // spans
    kv_local = cache_keys.shape[2] // HD
    head_count = queries.shape[1] // HD
    group_size = head_count // kv_local
    local_req = span_req % spans
    lengths = cache_len[local_req]
    queries_split = queries.reshape(spans, length, kv_local, group_size, HD)
    own_keys = new_keys.reshape(spans, length, kv_local, HD)
    own_values = new_values.reshape(spans, length, kv_local, HD)
    keys_cached = cache_keys[local_req].reshape(spans, cache_size, kv_local, HD)
    values_cached = cache_values[local_req].reshape(spans, cache_size, kv_local, HD)
    all_keys = jnp.concatenate([keys_cached, own_keys], axis=1)
    all_values = jnp.concatenate([values_cached, own_values], axis=1)
    scores = jnp.einsum(
        "clgqd,ckgd->cgqlk", queries_split, all_keys, preferred_element_type=jnp.float32
    ) * (1.0 / math.sqrt(HD))
    key_pos = jnp.arange(cache_size + length, dtype=jnp.int32)
    query_pos = jnp.arange(length, dtype=jnp.int32)
    in_cache = key_pos[None, None, :] < lengths[:, None, None]
    own_seen = key_pos[None, None, :] - cache_size <= query_pos[None, :, None]
    visible = jnp.where(key_pos[None, None, :] < cache_size, in_cache, own_seen)
    scores = jnp.where(visible[:, None, None], scores, negative_fill)
    weights = jax.nn.softmax(scores, axis=-1).astype(jnp.bfloat16)
    attended = jnp.einsum(
        "cgqlk,ckgd->clgqd", weights, all_values, preferred_element_type=jnp.float32
    )
    return attended.astype(jnp.bfloat16).reshape(spans * length, head_count * HD)


def routed_mix(normed, routes, gates, w_gate, w_up, w_down, capacity, experts):
    own_rows, model_width = normed.shape
    top_count = routes.shape[1]
    flat_routes = routes.reshape(-1)
    one_hot = (flat_routes[:, None] == jnp.arange(experts, dtype=jnp.int32)[None, :]).astype(
        jnp.int32
    )
    earlier = jnp.cumsum(one_hot, axis=0) - one_hot
    slot_index = jnp.sum(earlier * one_hot, axis=1)
    slot_target = flat_routes * capacity + slot_index
    pair_token = jnp.arange(flat_routes.shape[0], dtype=jnp.int32) // top_count
    source_row = (
        jnp.full((experts * capacity,), own_rows, jnp.int32).at[slot_target].set(pair_token)
    )
    padded_rows = jnp.concatenate([normed, jnp.zeros((1, model_width), jnp.bfloat16)], axis=0)
    outgoing = padded_rows[source_row].reshape(experts, capacity, model_width)
    slot_block = lax.all_to_all(
        outgoing, ("expert", "attn"), split_axis=0, concat_axis=0, tiled=True
    )
    rows_in = slot_block.reshape(-1, model_width)
    gate_part = jnp.dot(rows_in, w_gate[0], preferred_element_type=jnp.float32)
    up_part = jnp.dot(rows_in, w_up[0], preferred_element_type=jnp.float32)
    act = (jax.nn.silu(gate_part) * up_part).astype(jnp.bfloat16)
    expert_out = jnp.dot(act, w_down[0], preferred_element_type=jnp.float32).astype(jnp.bfloat16)
    computed = expert_out.reshape(slot_block.shape)
    returned = lax.all_to_all(computed, ("expert", "attn"), split_axis=0, concat_axis=0, tiled=True)
    picked = returned.reshape(experts * capacity, model_width)[slot_target].astype(jnp.float32)
    weight = gates / jnp.sum(gates, axis=-1, keepdims=True)
    return jnp.sum(
        (picked * weight.reshape(-1, 1)).reshape(own_rows, top_count, model_width), axis=1
    )


def routed_layer(
    queries,
    new_keys,
    new_values,
    cache_keys,
    cache_values,
    cache_len,
    span_req,
    out_proj,
    resid,
    norm_gain,
    routes,
    gates,
    w_gate,
    w_up,
    w_down,
):
    experts = lax.axis_size("expert") * lax.axis_size("attn")
    capacity = 2 * routes.shape[1] * resid.shape[0] // experts
    attended = attend(
        queries, new_keys, new_values, cache_keys, cache_values, cache_len, span_req
    )
    attn_out = lax.psum_scatter(
        jnp.dot(attended, out_proj, preferred_element_type=jnp.float32),
        "attn",
        scatter_dimension=0,
        tiled=True,
    )
    hidden = (resid.astype(jnp.float32) + attn_out).astype(jnp.bfloat16)
    state_float = hidden.astype(jnp.float32)
    mean_square = jnp.mean(state_float * state_float, axis=-1, keepdims=True)
    normed = (state_float * lax.rsqrt(mean_square + 1e-06) * norm_gain).astype(jnp.bfloat16)
    mixed = routed_mix(normed, routes, gates, w_gate, w_up, w_down, capacity, experts)
    return (state_float + mixed).astype(jnp.bfloat16)


def per_device(*args):
    cache_keys, routes = args[3], args[10]
    n_expert, n_attn = lax.axis_size("expert"), lax.axis_size("attn")
    everywhere = 2 * routes.shape[1] >= n_expert * n_attn
    fits = n_attn == 2 and n_expert > 2 and n_expert & (n_expert - 1) == 0
    fits = fits and cache_keys.shape[0] == 2 and cache_keys.shape[2] == HD
    if everywhere and fits:
        return dense_layer(*args)
    return routed_layer(*args)


def solution(mesh):
    placed = (
        P(("groups", "expert"), "attn"),
        P(("groups", "expert"), "attn"),
        P(("groups", "expert"), "attn"),
        P(("groups", "expert"), None, "attn"),
        P(("groups", "expert"), None, "attn"),
        P(("groups", "expert")),
        P(("groups", "expert")),
        P("attn", None),
        P(("groups", "expert", "attn"), None),
        P(),
        P(("groups", "expert", "attn"), None),
        P(("groups", "expert", "attn"), None),
        P(("expert", "attn"), None, None),
        P(("expert", "attn"), None, None),
        P(("expert", "attn"), None, None),
    )
    return jax.shard_map(
        per_device,
        mesh=mesh,
        in_specs=placed,
        out_specs=P(("groups", "expert", "attn"), None),
        check_vma=False,
    )
```
